32 devices in a mesh: grp: 2 (over y), row: 4 (over z), col: 4 (over x, core).
Axes of the slice: x: 2, y: 2, z: 4, core: 2. Of those that a mesh axis runs over, the one named last changes fastest.
Arguments:
- src_raw: bfloat16 [8, 2, 512, 1024], P(('grp', 'row'), None, 'col'), parts along dimension 0, may hold values from -36 to 36
- block_owner: int32 [4, 4], P('grp', 'col'), parts along dimension 0, may hold values from 0 to 3, as said below
- chan_order: int32 [4, 4, 128], P('grp', 'col'), parts along dimension 0, may hold values from 0 to 127, each once within a row
- rec_raw: bfloat16 [4, 16, 1024], P('grp', ('row', 'col')), parts along dimension 0, may hold values from -36 to 36
- fir_taps: bfloat16 [129], replicated, may hold values from -0.5 to 0.5
- stacks: float32 [1024, 1024], P(('grp', 'col'), 'row'), parts along dimension 0, may hold values from -6 to 6
Outputs:
- new_stacks: float32 [1024, 1024], P(('grp', 'col'), 'row'), parts along dimension 0
The draws below stay inside these ranges and needn't reach their ends.
There are 2 independent parts, one for each index of `grp`. The reference program is written for one: setup_inputs(seed, part) draws one part's arguments, and reference() takes and returns one part's arrays. A program takes and returns all parts, laid end to end along the dimension named above; an argument that names none is the same for every part. Nothing has to cross between parts.
Inputs may be any that keep to these rules, and one draw needn't show every extreme that they name: block_owner[w, c] is the row index whose buffer holds column block c's traces in window w; 0 and 3 both occur in every draw.
All inputs are finite; a program needn't handle non-finite values.
Results may differ from the reference program's by a relative error of at most 0.0018.
Values may be sent and summed in bfloat16 or wider, within the bound.
No kernel may reach another device: no remote copies, remote signals or barrier semaphores. Data moves between devices by JAX's collectives and lax.ppermute only.
A program may use at most 64 MiB of HBM per device.

```python
import math
import jax
import jax.numpy as jnp
from jax import lax

L = 1024
W = 2
TAPS = 129
LAGS = 64
BLK = 128
S = 512
QROW = 4
OWNERS = 4
R = 16
N_COL = 4


def draw_src_raw(key, part):
    sub_keys = jax.random.split(jax.random.fold_in(key, 11), 3)
    full_shape = (OWNERS, W, S, L)
    chan_scale = jnp.exp(jax.random.uniform(sub_keys[0], (1, 1, S, 1), jnp.float32, jnp.log(0.3), jnp.log(3.0)))
    time_scale = jnp.exp(jax.random.uniform(sub_keys[1], (1, W, 1, L), jnp.float32, jnp.log(0.3), jnp.log(3.0)))
    noise_field = jnp.clip(jax.random.normal(sub_keys[2], full_shape, jnp.float32), -4.0, 4.0)
    return (noise_field * chan_scale * time_scale).astype(jnp.bfloat16)


def draw_rec_raw(key, part):
    sub_keys = jax.random.split(jax.random.fold_in(key, 23), 3)
    full_shape = (W, R, L)
    chan_scale = jnp.exp(jax.random.uniform(sub_keys[0], (1, R, 1), jnp.float32, jnp.log(0.3), jnp.log(3.0)))
    time_scale = jnp.exp(jax.random.uniform(sub_keys[1], (W, 1, L), jnp.float32, jnp.log(0.3), jnp.log(3.0)))
    noise_field = jnp.clip(jax.random.normal(sub_keys[2], full_shape, jnp.float32), -4.0, 4.0)
    return (noise_field * chan_scale * time_scale).astype(jnp.bfloat16)


def draw_block_owner(key, part):
    sub_keys = jax.random.split(jax.random.fold_in(key, 37), 2)
    total = W * N_COL
    owners_flat = jax.random.randint(sub_keys[0], (total,), 0, OWNERS)
    positions = jax.random.permutation(sub_keys[1], total)
    owners_flat = owners_flat.at[positions[0]].set(0)
    owners_flat = owners_flat.at[positions[1]].set(OWNERS - 1)
    return owners_flat.reshape((W, N_COL)).astype(jnp.int32)


def level_of(own_key, extent, shards, least, largest):
    def one(axis_at, blocks):
        heights = jax.random.uniform(jax.random.fold_in(jax.random.fold_in(own_key, 6), axis_at), (blocks,), jnp.float32, least / len(shards), largest / len(shards))
        return jnp.repeat(jnp.exp(heights), extent[axis_at] // blocks).reshape((-1,) + (1,) * (len(extent) - axis_at - 1))

    level = one(*shards[0])
    for cut in shards[1:]:
        level = level * one(*cut)
    return level


def centred(key, dims, spread, most, cuts=(), kind=jnp.bfloat16):
    array = jax.random.normal(key, dims, jnp.float32) * spread
    if len(cuts) > 0:
        array = level_of(key, dims, cuts, -0.22, 0.18) * array
    return jnp.clip(array, min=-most, max=most).astype(kind)


def setup_inputs(seed: int = 0, part: int = 0) -> dict:
    arg_keys = jax.random.split(jax.random.key(seed), 7)
    own_keys = jax.random.split(jax.random.fold_in(arg_keys[6], part), 7)
    src_raw = draw_src_raw(jax.random.fold_in(jax.random.fold_in(arg_keys[6], part), 71), part)
    block_owner = draw_block_owner(jax.random.fold_in(jax.random.fold_in(arg_keys[6], part), 71), part)
    chan_order = jax.vmap(lambda own: jax.random.permutation(own, BLK))(jax.random.split(own_keys[2], W * N_COL)).reshape((W, N_COL, BLK)).astype(jnp.int32)
    rec_raw = draw_rec_raw(jax.random.fold_in(jax.random.fold_in(arg_keys[6], part), 71), part)
    fir_taps = centred(arg_keys[4], (TAPS,), TAPS ** -0.5, 0.5)
    stacks = centred(own_keys[5], (S, R * LAGS), 1.0, 6.0, ((0, 4), (1, 4)), jnp.float32)
    return {"src_raw": src_raw, "block_owner": block_owner, "chan_order": chan_order, "rec_raw": rec_raw, "fir_taps": fir_taps, "stacks": stacks}


def apply_filter(raw, fir_taps):
    half_taps = (TAPS - 1) // 2
    padded = jnp.pad(raw.astype(jnp.float32), [(0, 0)] * (raw.ndim - 1) + [(half_taps, half_taps)])
    tap_values = fir_taps.astype(jnp.float32)
    result = jnp.zeros(raw.shape, jnp.float32)
    for offset in range(TAPS):
        result = result + tap_values[offset] * padded[..., offset:offset + L]
    return result.astype(jnp.bfloat16)

def pair_terms(source_rows, src_energy, rec_rows):
    count = rec_rows.shape[0]
    half_lags = LAGS // 2
    padded = jnp.pad(rec_rows.astype(jnp.float32), ((0, 0), (half_lags, LAGS - half_lags)))
    hankel = jnp.stack([padded[:, offset:offset + L] for offset in range(LAGS)], axis=1)
    hankel = hankel.reshape((count * LAGS, L))
    lagged = jnp.dot(source_rows.astype(jnp.float32), hankel.T, precision=lax.Precision.HIGHEST)
    rec_energy = lax.optimization_barrier(jnp.sum(jnp.square(rec_rows.astype(jnp.float32)), axis=1))
    scale_pair = lax.rsqrt(src_energy[:, None, None] * rec_energy[None, :, None] + 1e-06)
    ratio = lagged.reshape((source_rows.shape[0], count, LAGS)) * scale_pair
    return jnp.tanh(0.5 * math.sqrt(L) * ratio).reshape((source_rows.shape[0], count * LAGS))

def reference(src_raw, block_owner, chan_order, rec_raw, fir_taps, stacks):
    receivers = apply_filter(rec_raw, fir_taps)
    updated = stacks
    for window in range(W):
        blocks = []
        for column in range(S // BLK):
            owner_row = block_owner[window, column].astype(jnp.int32)
            owner_rows = lax.dynamic_index_in_dim(src_raw, owner_row, 0, keepdims=False)
            block_rows = owner_rows[window, column * BLK:(column + 1) * BLK]
            blocks.append(jnp.take(block_rows, chan_order[window, column].astype(jnp.int32), axis=0))
        sources = apply_filter(jnp.concatenate(blocks, axis=0), fir_taps)
        src_energy = lax.optimization_barrier(jnp.sum(jnp.square(sources.astype(jnp.float32)), axis=1))
        rec_groups = receivers[window].reshape((R // QROW, QROW, L))
        terms = lax.map(lambda rec_rows: pair_terms(sources, src_energy, rec_rows), rec_groups)
        updated = updated + jnp.transpose(terms, (1, 0, 2)).reshape((S, R * LAGS))
    return updated
```

```python
import functools
import math

import jax
import jax.numpy as jnp
from jax import lax
from jax.experimental import pallas as pl
from jax.experimental.pallas import tpu as pltpu
from jax.sharding import PartitionSpec as P

LAGS = 64
LANES = 128
DIRECT_ROWS = 8
VMEM_GRANT = 16 * 2**20
VMEM = pl.BlockSpec(memory_space=pltpu.VMEM)
SMEM = pl.BlockSpec(memory_space=pltpu.SMEM)


def dot_nt(left, right):
    return lax.dot_general(left, right, (((1,), (1,)), ((), ())), preferred_element_type=jnp.float32)


def filter_rows(raw, band):
    blocks = raw.shape[1] // LANES
    halo = (band.shape[1] // LANES - 1) // 2
    out = []
    for block in range(blocks):
        low, high = max(block - halo, 0), min(block + halo + 1, blocks)
        first = low - (block - halo)
        taps = band[:, first * LANES : (first + high - low) * LANES]
        out.append(dot_nt(raw[:, low * LANES : high * LANES], taps))
    return jnp.concatenate(out[::-1], axis=1)


def source_kernel(owner_ref, order_ref, raw_ref, taps_ref, kept_ref, energy_ref, band_ref, row_ref):
    taps = taps_ref.shape[1]
    half = (taps - 1) // 2
    halo = pl.cdiv(half, LANES)
    row_ref[...] = jnp.zeros_like(row_ref)
    row_ref[:, 0:taps] = taps_ref[...].astype(jnp.float32)
    spread = jnp.broadcast_to(row_ref[...], (LANES, row_ref.shape[1]))
    band = pltpu.roll(spread, halo * LANES - half, 1, stride=1, stride_axis=0).astype(jnp.bfloat16)
    across = lax.broadcasted_iota(jnp.int32, (LANES, LANES), 0)
    down = lax.broadcasted_iota(jnp.int32, (LANES, LANES), 1)
    mirror = jnp.where(across + down == LANES - 1, 1.0, 0.0).astype(jnp.bfloat16)
    band = jnp.dot(mirror, band, preferred_element_type=jnp.float32).astype(jnp.bfloat16)
    band_ref[...] = band
    here = lax.axis_index("row")
    windows, count, _ = kept_ref.shape
    for window in range(windows):
        place = lax.broadcasted_iota(jnp.int32, (count, count), 0)
        order = jnp.where(owner_ref[window, 0] == here, order_ref[window], -1)
        chosen = jnp.where(place == order, 1.0, 0.0).T.astype(jnp.bfloat16)
        raw = jnp.dot(chosen, raw_ref[window], preferred_element_type=jnp.float32)
        kept = filter_rows(raw.astype(jnp.bfloat16), band).astype(jnp.bfloat16)
        kept_ref[window] = kept
        squares = jnp.square(kept.astype(jnp.float32))
        energy_ref[window] = jnp.sum(squares, axis=1, keepdims=True)


def prepare_sources(block_owner, chan_order, raw, fir_taps):
    windows, count, length = raw.shape
    taps = fir_taps.shape[0]
    width = LANES * (2 * pl.cdiv((taps - 1) // 2, LANES) + 1)
    return pl.pallas_call(
        source_kernel,
        out_shape=(
            jax.ShapeDtypeStruct((windows, count, length), jnp.bfloat16),
            jax.ShapeDtypeStruct((windows, count, 1), jnp.float32),
            jax.ShapeDtypeStruct((LANES, width), jnp.bfloat16),
        ),
        in_specs=[SMEM, VMEM, VMEM, VMEM],
        out_specs=(VMEM, VMEM, VMEM),
        scratch_shapes=[pltpu.VMEM((1, width), jnp.float32)],
        cost_estimate=pl.CostEstimate(
            flops=2 * windows * count * length * (count + width),
            bytes_accessed=4 * windows * count * length,
            transcendentals=0,
        ),
        compiler_params=pltpu.CompilerParams(vmem_limit_bytes=VMEM_GRANT),
        name="prepare_sources",
    )(block_owner, chan_order, raw, fir_taps.reshape(1, taps))


def pair_kernel(rec_ref, band_ref, kept_ref, energy_ref, out_ref, hankel_ref):
    receivers, windows, length = rec_ref.shape
    rows = receivers * windows
    raw = jnp.concatenate([rec_ref[q].astype(jnp.float32) for q in range(receivers)], axis=0)
    rec = filter_rows(raw.astype(jnp.bfloat16), band_ref[...])
    rec = rec.astype(jnp.bfloat16).astype(jnp.float32)
    rec_energy = jnp.sum(jnp.square(rec), axis=1, keepdims=True)
    padded = jnp.concatenate([rec, jnp.zeros((rows, LANES), jnp.float32)], axis=1)
    width = length + LANES
    for window in range(windows):
        for q in range(receivers):
            at = q * windows + window
            spread = jnp.broadcast_to(padded[at : at + 1], (LAGS, width))
            shifted = pltpu.roll(spread, width - LAGS // 2, 1, stride=1, stride_axis=0)
            hankel_ref[window, q * LAGS : (q + 1) * LAGS] = shifted[:, :length].astype(jnp.bfloat16)
    lane = lax.broadcasted_iota(jnp.int32, (rows, receivers * LAGS), 1) // LAGS
    row = lax.broadcasted_iota(jnp.int32, (rows, receivers * LAGS), 0)
    total = None
    for window in range(windows):
        own = jnp.where(row == lane * windows + window, rec_energy, 0.0)
        across = jnp.sum(own, axis=0, keepdims=True)
        lagged = dot_nt(kept_ref[window], hankel_ref[window])
        ratio = lagged * lax.rsqrt(energy_ref[window] * across + 1e-06)
        term = jnp.tanh(0.5 * math.sqrt(length) * ratio)
        total = term if total is None else total + term
    out_ref[...] = total.astype(out_ref.dtype)


def pair_terms(rec, band, kept, energy, dtype):
    receivers, windows, length = rec.shape
    count = kept.shape[1]
    return pl.pallas_call(
        pair_kernel,
        out_shape=jax.ShapeDtypeStruct((count, receivers * LAGS), dtype),
        in_specs=[VMEM] * 4,
        out_specs=VMEM,
        scratch_shapes=[pltpu.VMEM((windows, receivers * LAGS, length), jnp.bfloat16)],
        cost_estimate=pl.CostEstimate(
            flops=2 * windows * count * length * receivers * LAGS,
            bytes_accessed=4 * windows * count * length,
            transcendentals=windows * count * receivers * LAGS,
        ),
        compiler_params=pltpu.CompilerParams(vmem_limit_bytes=VMEM_GRANT),
        name="pair_terms",
    )(rec, band, kept, energy)


def gather_columns(piece, columns):
    here = lax.axis_index("col")
    if columns & (columns - 1):
        return lax.all_gather(piece, "col", axis=0, tiled=True)
    bit = 1
    while bit < columns:
        other = lax.ppermute(piece, "col", [(i, i ^ bit) for i in range(columns)])
        mine_first = (here & bit) == 0
        piece = jnp.concatenate(
            [jnp.where(mine_first, piece, other), jnp.where(mine_first, other, piece)], axis=0
        )
        bit *= 2
    return piece


def shards(mesh_shape, src_raw, block_owner, chan_order, rec_raw, fir_taps, stacks):
    rows, columns = mesh_shape["row"], mesh_shape["col"]
    kept, energy, band = prepare_sources(block_owner, chan_order, src_raw[0], fir_taps)
    receivers = gather_columns(jnp.swapaxes(rec_raw, 0, 1), columns)
    terms = functools.partial(pair_terms, band=band, kept=kept, energy=energy)
    if rows > DIRECT_ROWS:
        everyone = lax.all_gather(receivers, "row", axis=0)
        parts = lax.map(lambda rec: terms(rec, dtype=jnp.bfloat16), everyone)
        parts = lax.all_to_all(parts, "row", 0, 0, tiled=True)
        return stacks + jnp.sum(parts.astype(jnp.float32), axis=0)

    def partner(i, step):
        return i ^ step if rows & (rows - 1) == 0 else (i + step) % rows

    order = range(rows - 1, 0, -1)
    arrived = {}
    for step in order:
        pairs = [(partner(i, step), i) for i in range(rows)]
        arrived[step] = lax.ppermute(receivers, "row", pairs)
    parts = []
    for step in order:
        pairs = [(i, partner(i, step)) for i in range(rows)]
        parts.append(lax.ppermute(terms(arrived[step], dtype=jnp.bfloat16), "row", pairs))
    total = stacks + terms(receivers, dtype=jnp.float32)
    for part in parts:
        total = total + part.astype(jnp.float32)
    return total


def solution(mesh):
    in_specs = (
        P(("grp", "row"), None, "col", None),
        P("grp", "col"),
        P("grp", "col", None),
        P("grp", ("row", "col"), None),
        P(),
        P(("grp", "col"), "row"),
    )
    out_specs = P(("grp", "col"), "row")
    body = functools.partial(shards, dict(mesh.shape))
    return jax.shard_map(body, mesh=mesh, in_specs=in_specs, out_specs=out_specs, check_vma=False)
```

```python
import functools
import math

import jax
import jax.numpy as jnp
from jax import lax
from jax.experimental import pallas as pl
from jax.experimental.pallas import tpu as pltpu
from jax.sharding import PartitionSpec as P

LAGS = 64
LANES = 128
DIRECT_ROWS = 8
VMEM_GRANT = 16 * 2**20
VMEM = pl.BlockSpec(memory_space=pltpu.VMEM)
HBM = pl.BlockSpec(memory_space=pltpu.HBM)


def in_hbm(value):
    return pltpu.with_memory_space_constraint(value, pltpu.HBM)


def dot_nt(left, right):
    return lax.dot_general(left, right, (((1,), (1,)), ((), ())), preferred_element_type=jnp.float32)


def filter_rows(raw, band):
    rows, length = raw.shape
    block, width = band.shape
    halo = (width - block) // 2
    edge = jnp.zeros((rows, halo), raw.dtype)
    padded = jnp.concatenate([edge, raw, edge], axis=1)
    starts = range(0, length, block)
    stacked = jnp.concatenate([padded[:, start : start + width] for start in starts], axis=0)
    out = dot_nt(stacked.astype(jnp.bfloat16), band)
    pieces = [out[i * rows : (i + 1) * rows] for i in range(len(starts))]
    return jnp.concatenate(pieces[::-1], axis=1)


def source_kernel(
    owner_hbm,
    order_hbm,
    raw_hbm,
    taps_ref,
    kept_ref,
    energy_ref,
    band_ref,
    owner_ref,
    order_ref,
    raw_ref,
    row_ref,
    arrived,
):
    windows, count, _ = kept_ref.shape
    owner_copy = pltpu.make_async_copy(owner_hbm, owner_ref, arrived.at[windows])
    order_copy = pltpu.make_async_copy(order_hbm, order_ref, arrived.at[windows + 1])
    copies = [
        pltpu.make_async_copy(raw_hbm.at[window], raw_ref.at[window], arrived.at[window])
        for window in range(windows)
    ]
    for copy in (owner_copy, order_copy, *copies):
        copy.start()
    taps = taps_ref.shape[1]
    half = (taps - 1) // 2
    block, width = band_ref.shape
    row_ref[...] = jnp.zeros_like(row_ref)
    row_ref[:, 0:taps] = taps_ref[...].astype(jnp.float32)
    spread = jnp.broadcast_to(row_ref[...], (LANES, width - LANES))
    part = pltpu.roll(spread, (width - block) // 2 - half, 1, stride=1, stride_axis=0)
    across = lax.broadcasted_iota(jnp.int32, (LANES, LANES), 0)
    down = lax.broadcasted_iota(jnp.int32, (LANES, LANES), 1)
    mirror = jnp.where(across + down == LANES - 1, 1.0, 0.0).astype(jnp.bfloat16)
    part = jnp.dot(mirror, part.astype(jnp.bfloat16), preferred_element_type=jnp.float32)
    empty = jnp.zeros((LANES, LANES), jnp.float32)
    upper = jnp.concatenate([empty, part], axis=1)
    lower = jnp.concatenate([part, empty], axis=1)
    band = jnp.concatenate([upper, lower], axis=0).astype(jnp.bfloat16)
    band_ref[...] = band
    here = lax.axis_index("row")
    owner_copy.wait()
    order_copy.wait()
    for window in range(windows):
        place = lax.broadcasted_iota(jnp.int32, (count, count), 0)
        order = jnp.where(owner_ref[0, window] == here, order_ref[window], -1)
        chosen = jnp.where(place == order, 1.0, 0.0).T.astype(jnp.bfloat16)
        copies[window].wait()
        raw = jnp.dot(chosen, raw_ref[window], preferred_element_type=jnp.float32)
        kept = filter_rows(raw.astype(jnp.bfloat16), band).astype(jnp.bfloat16)
        kept_ref[window] = kept
        squares = jnp.square(kept.astype(jnp.float32))
        energy_ref[window] = jnp.sum(squares, axis=1, keepdims=True)


def prepare_sources(block_owner, chan_order, raw, fir_taps):
    windows, count, length = raw.shape
    taps = fir_taps.shape[0]
    block = 2 * LANES
    width = block + 2 * LANES * pl.cdiv((taps - 1) // 2, LANES)
    return pl.pallas_call(
        source_kernel,
        out_shape=(
            jax.ShapeDtypeStruct((windows, count, length), jnp.bfloat16),
            jax.ShapeDtypeStruct((windows, count, 1), jnp.float32),
            jax.ShapeDtypeStruct((block, width), jnp.bfloat16),
        ),
        in_specs=[HBM, HBM, HBM, VMEM],
        out_specs=(VMEM, VMEM, VMEM),
        scratch_shapes=[
            pltpu.SMEM((1, windows), jnp.int32),
            pltpu.VMEM((windows, 1, count), jnp.int32),
            pltpu.VMEM((windows, count, length), jnp.bfloat16),
            pltpu.VMEM((1, width - LANES), jnp.float32),
            pltpu.SemaphoreType.DMA((windows + 2,)),
        ],
        cost_estimate=pl.CostEstimate(
            flops=2 * windows * count * length * (count + width),
            bytes_accessed=4 * windows * count * length,
            transcendentals=0,
        ),
        compiler_params=pltpu.CompilerParams(vmem_limit_bytes=VMEM_GRANT),
        name="prepare_sources",
    )(in_hbm(block_owner.T), in_hbm(chan_order), in_hbm(raw), fir_taps.reshape(1, taps))


def pair_kernel(rec_ref, band_ref, kept_ref, energy_ref, out_ref, hankel_ref):
    receivers, windows, length = rec_ref.shape
    rows = receivers * windows
    raw = jnp.concatenate([rec_ref[q].astype(jnp.float32) for q in range(receivers)], axis=0)
    rec = filter_rows(raw, band_ref[...])
    rec = rec.astype(jnp.bfloat16).astype(jnp.float32)
    rec_energy = jnp.sum(jnp.square(rec), axis=1, keepdims=True)
    padded = jnp.concatenate([rec, jnp.zeros((rows, LANES), jnp.float32)], axis=1)
    width = length + LANES
    for window in range(windows):
        for q in range(receivers):
            at = q * windows + window
            spread = jnp.broadcast_to(padded[at : at + 1], (LAGS, width))
            shifted = pltpu.roll(spread, width - LAGS // 2, 1, stride=1, stride_axis=0)
            hankel_ref[window, q * LAGS : (q + 1) * LAGS] = shifted[:, :length].astype(jnp.bfloat16)
    lane = lax.broadcasted_iota(jnp.int32, (rows, receivers * LAGS), 1) // LAGS
    row = lax.broadcasted_iota(jnp.int32, (rows, receivers * LAGS), 0)
    total = None
    for window in range(windows):
        own = jnp.where(row == lane * windows + window, rec_energy, 0.0)
        across = jnp.sum(own, axis=0, keepdims=True)
        lagged = dot_nt(kept_ref[window], hankel_ref[window])
        ratio = lagged * lax.rsqrt(energy_ref[window] * across + 1e-06)
        term = jnp.tanh(0.5 * math.sqrt(length) * ratio)
        total = term if total is None else total + term
    out_ref[...] = total.astype(out_ref.dtype)


def pair_terms(rec, band, kept, energy, dtype):
    receivers, windows, length = rec.shape
    count = kept.shape[1]
    return pl.pallas_call(
        pair_kernel,
        out_shape=jax.ShapeDtypeStruct((count, receivers * LAGS), dtype),
        in_specs=[VMEM] * 4,
        out_specs=VMEM,
        scratch_shapes=[pltpu.VMEM((windows, receivers * LAGS, length), jnp.bfloat16)],
        cost_estimate=pl.CostEstimate(
            flops=2 * windows * count * length * receivers * LAGS,
            bytes_accessed=4 * windows * count * length,
            transcendentals=windows * count * receivers * LAGS,
        ),
        compiler_params=pltpu.CompilerParams(vmem_limit_bytes=VMEM_GRANT),
        name="pair_terms",
    )(rec, band, kept, energy)


def gather_columns(piece, columns):
    here = lax.axis_index("col")
    if columns & (columns - 1):
        return lax.all_gather(piece, "col", axis=0, tiled=True)
    bit = 1
    while bit < columns:
        other = lax.ppermute(piece, "col", [(i, i ^ bit) for i in range(columns)])
        mine_first = (here & bit) == 0
        piece = jnp.concatenate(
            [jnp.where(mine_first, piece, other), jnp.where(mine_first, other, piece)], axis=0
        )
        bit *= 2
    return piece


def shards(mesh_shape, src_raw, block_owner, chan_order, rec_raw, fir_taps, stacks):
    rows, columns = mesh_shape["row"], mesh_shape["col"]
    kept, energy, band = prepare_sources(block_owner, chan_order, src_raw[0], fir_taps)
    receivers = gather_columns(jnp.swapaxes(rec_raw, 0, 1), columns)
    receivers, kept, energy, band = lax.optimization_barrier((receivers, kept, energy, band))
    terms = functools.partial(pair_terms, band=band, kept=kept, energy=energy)
    if rows > DIRECT_ROWS:
        everyone = lax.all_gather(receivers, "row", axis=0)
        parts = lax.map(lambda rec: terms(rec, dtype=jnp.bfloat16), everyone)
        parts = lax.all_to_all(parts, "row", 0, 0, tiled=True)
        return stacks + jnp.sum(parts.astype(jnp.float32), axis=0)

    def partner(i, step):
        return i ^ step if rows & (rows - 1) == 0 else (i + step) % rows

    order = [1, *range(rows - 1, 1, -1)]
    arrived = {}
    for step in order:
        pairs = [(partner(i, step), i) for i in range(rows)]
        arrived[step] = lax.ppermute(receivers, "row", pairs)
    parts = []
    for step in order:
        pairs = [(i, partner(i, step)) for i in range(rows)]
        parts.append(lax.ppermute(terms(arrived[step], dtype=jnp.bfloat16), "row", pairs))
    total = stacks + terms(receivers, dtype=jnp.float32)
    for part in parts:
        total = total + part.astype(jnp.float32)
    return total


def solution(mesh):
    in_specs = (
        P(("grp", "row"), None, "col", None),
        P("grp", "col"),
        P("grp", "col", None),
        P("grp", ("row", "col"), None),
        P(),
        P(("grp", "col"), "row"),
    )
    out_specs = P(("grp", "col"), "row")
    body = functools.partial(shards, dict(mesh.shape))
    return jax.shard_map(body, mesh=mesh, in_specs=in_specs, out_specs=out_specs, check_vma=False)
```

```python
import functools
import math

import jax
import jax.numpy as jnp
from jax import lax
from jax.experimental import pallas as pl
from jax.experimental.pallas import tpu as pltpu
from jax.sharding import PartitionSpec as P

LAGS = 64
LANES = 128
DIRECT_ROWS = 8
VMEM_GRANT = 16 * 2**20
VMEM = pl.BlockSpec(memory_space=pltpu.VMEM)
HBM = pl.BlockSpec(memory_space=pltpu.HBM)


def in_hbm(value):
    return pltpu.with_memory_space_constraint(value, pltpu.HBM)


def dot_nt(left, right):
    return lax.dot_general(left, right, (((1,), (1,)), ((), ())), preferred_element_type=jnp.float32)


def filter_rows(raw, band):
    rows, length = raw.shape
    block, width = band.shape
    halo = (width - block) // 2
    edge = jnp.zeros((rows, halo), raw.dtype)
    padded = jnp.concatenate([edge, raw, edge], axis=1)
    starts = range(0, length, block)
    stacked = jnp.concatenate([padded[:, start : start + width] for start in starts], axis=0)
    out = dot_nt(stacked.astype(jnp.bfloat16), band)
    pieces = [out[i * rows : (i + 1) * rows] for i in range(len(starts))]
    return jnp.concatenate(pieces[::-1], axis=1)


def source_kernel(
    owner_hbm,
    order_hbm,
    raw_hbm,
    taps_ref,
    kept_ref,
    energy_ref,
    band_ref,
    owner_ref,
    order_ref,
    raw_ref,
    row_ref,
    arrived,
):
    windows, count, _ = kept_ref.shape
    owner_copy = pltpu.make_async_copy(owner_hbm, owner_ref, arrived.at[windows])
    order_copy = pltpu.make_async_copy(order_hbm, order_ref, arrived.at[windows + 1])
    copies = [
        pltpu.make_async_copy(raw_hbm.at[window], raw_ref.at[window], arrived.at[window])
        for window in range(windows)
    ]
    for copy in (owner_copy, order_copy, *copies):
        copy.start()
    taps = taps_ref.shape[1]
    half = (taps - 1) // 2
    block, width = band_ref.shape
    row_ref[...] = jnp.zeros_like(row_ref)
    row_ref[:, 0:taps] = taps_ref[...].astype(jnp.float32)
    spread = jnp.broadcast_to(row_ref[...], (LANES, width - LANES))
    part = pltpu.roll(spread, (width - block) // 2 - half, 1, stride=1, stride_axis=0)
    across = lax.broadcasted_iota(jnp.int32, (LANES, LANES), 0)
    down = lax.broadcasted_iota(jnp.int32, (LANES, LANES), 1)
    mirror = jnp.where(across + down == LANES - 1, 1.0, 0.0).astype(jnp.bfloat16)
    part = jnp.dot(mirror, part.astype(jnp.bfloat16), preferred_element_type=jnp.float32)
    empty = jnp.zeros((LANES, LANES), jnp.float32)
    upper = jnp.concatenate([empty, part], axis=1)
    lower = jnp.concatenate([part, empty], axis=1)
    band = jnp.concatenate([upper, lower], axis=0).astype(jnp.bfloat16)
    band_ref[...] = band
    here = lax.axis_index("row")
    owner_copy.wait()
    order_copy.wait()
    for window in range(windows):
        place = lax.broadcasted_iota(jnp.int32, (count, count), 0)
        order = jnp.where(owner_ref[0, window] == here, order_ref[window], -1)
        chosen = jnp.where(place == order, 1.0, 0.0).T.astype(jnp.bfloat16)
        copies[window].wait()
        raw = jnp.dot(chosen, raw_ref[window], preferred_element_type=jnp.float32)
        kept = filter_rows(raw.astype(jnp.bfloat16), band).astype(jnp.bfloat16)
        kept_ref[window] = kept
        squares = jnp.square(kept.astype(jnp.float32))
        energy_ref[window] = jnp.sum(squares, axis=1, keepdims=True)


def prepare_sources(block_owner, chan_order, raw, fir_taps):
    windows, count, length = raw.shape
    taps = fir_taps.shape[0]
    block = 2 * LANES
    width = block + 2 * LANES * pl.cdiv((taps - 1) // 2, LANES)
    return pl.pallas_call(
        source_kernel,
        out_shape=(
            jax.ShapeDtypeStruct((windows, count, length), jnp.bfloat16),
            jax.ShapeDtypeStruct((windows, count, 1), jnp.float32),
            jax.ShapeDtypeStruct((block, width), jnp.bfloat16),
        ),
        in_specs=[HBM, HBM, HBM, VMEM],
        out_specs=(VMEM, VMEM, VMEM),
        scratch_shapes=[
            pltpu.SMEM((1, windows), jnp.int32),
            pltpu.VMEM((windows, 1, count), jnp.int32),
            pltpu.VMEM((windows, count, length), jnp.bfloat16),
            pltpu.VMEM((1, width - LANES), jnp.float32),
            pltpu.SemaphoreType.DMA((windows + 2,)),
        ],
        cost_estimate=pl.CostEstimate(
            flops=2 * windows * count * length * (count + width),
            bytes_accessed=4 * windows * count * length,
            transcendentals=0,
        ),
        compiler_params=pltpu.CompilerParams(vmem_limit_bytes=VMEM_GRANT),
        name="prepare_sources",
    )(in_hbm(block_owner.T), in_hbm(chan_order), in_hbm(raw), fir_taps.reshape(1, taps))


def pair_kernel(rec_ref, band_ref, kept_ref, energy_ref, out_ref, hankel_ref):
    receivers, windows, length = rec_ref.shape
    rows = receivers * windows
    raw = jnp.concatenate([rec_ref[q].astype(jnp.float32) for q in range(receivers)], axis=0)
    rec = filter_rows(raw, band_ref[...])
    rec = rec.astype(jnp.bfloat16).astype(jnp.float32)
    rec_energy = jnp.sum(jnp.square(rec), axis=1, keepdims=True)
    padded = jnp.concatenate([rec, jnp.zeros((rows, LANES), jnp.float32)], axis=1)
    width = length + LANES
    for window in range(windows):
        for q in range(receivers):
            at = q * windows + window
            spread = jnp.broadcast_to(padded[at : at + 1], (LAGS, width))
            shifted = pltpu.roll(spread, width - LAGS // 2, 1, stride=1, stride_axis=0)
            hankel_ref[window, q * LAGS : (q + 1) * LAGS] = shifted[:, :length].astype(jnp.bfloat16)
    lane = lax.broadcasted_iota(jnp.int32, (rows, receivers * LAGS), 1) // LAGS
    row = lax.broadcasted_iota(jnp.int32, (rows, receivers * LAGS), 0)
    total = None
    for window in range(windows):
        own = jnp.where(row == lane * windows + window, rec_energy, 0.0)
        across = jnp.sum(own, axis=0, keepdims=True)
        lagged = dot_nt(kept_ref[window], hankel_ref[window])
        ratio = lagged * lax.rsqrt(energy_ref[window] * across + 1e-06)
        term = jnp.tanh(0.5 * math.sqrt(length) * ratio)
        total = term if total is None else total + term
    out_ref[...] = total.astype(out_ref.dtype)


def pair_terms(rec, band, kept, energy, dtype):
    receivers, windows, length = rec.shape
    count = kept.shape[1]
    return pl.pallas_call(
        pair_kernel,
        out_shape=jax.ShapeDtypeStruct((count, receivers * LAGS), dtype),
        in_specs=[VMEM] * 4,
        out_specs=VMEM,
        scratch_shapes=[pltpu.VMEM((windows, receivers * LAGS, length), jnp.bfloat16)],
        cost_estimate=pl.CostEstimate(
            flops=2 * windows * count * length * receivers * LAGS,
            bytes_accessed=4 * windows * count * length,
            transcendentals=windows * count * receivers * LAGS,
        ),
        compiler_params=pltpu.CompilerParams(vmem_limit_bytes=VMEM_GRANT),
        name="pair_terms",
    )(rec, band, kept, energy)


def gather_columns(piece, columns):
    here = lax.axis_index("col")
    if columns & (columns - 1):
        return lax.all_gather(piece, "col", axis=0, tiled=True)
    found = {0: piece}
    for step in range(columns - 1, 0, -1):
        found[step] = lax.ppermute(piece, "col", [(i, i ^ step) for i in range(columns)])
    pieces = [found[step] for step in range(columns)]
    bit = 1
    while bit < columns:
        flip = (here & bit) != 0
        pieces = [jnp.where(flip, pieces[i ^ bit], pieces[i]) for i in range(columns)]
        bit *= 2
    return jnp.concatenate(pieces, axis=0)


def shards(mesh_shape, src_raw, block_owner, chan_order, rec_raw, fir_taps, stacks):
    rows, columns = mesh_shape["row"], mesh_shape["col"]
    kept, energy, band = prepare_sources(block_owner, chan_order, src_raw[0], fir_taps)
    receivers = gather_columns(jnp.swapaxes(rec_raw, 0, 1), columns)
    receivers, kept, energy, band = lax.optimization_barrier((receivers, kept, energy, band))
    terms = functools.partial(pair_terms, band=band, kept=kept, energy=energy)
    if rows > DIRECT_ROWS:
        everyone = lax.all_gather(receivers, "row", axis=0)
        parts = lax.map(lambda rec: terms(rec, dtype=jnp.bfloat16), everyone)
        parts = lax.all_to_all(parts, "row", 0, 0, tiled=True)
        return stacks + jnp.sum(parts.astype(jnp.float32), axis=0)

    def partner(i, step):
        return i ^ step if rows & (rows - 1) == 0 else (i + step) % rows

    order = [1, *range(rows - 1, 1, -1)]
    arrived = {}
    for step in order:
        pairs = [(partner(i, step), i) for i in range(rows)]
        arrived[step] = lax.ppermute(receivers, "row", pairs)
    parts = []
    for step in order:
        pairs = [(i, partner(i, step)) for i in range(rows)]
        parts.append(lax.ppermute(terms(arrived[step], dtype=jnp.bfloat16), "row", pairs))
    total = stacks + terms(receivers, dtype=jnp.float32)
    for part in parts:
        total = total + part.astype(jnp.float32)
    return total


def solution(mesh):
    in_specs = (
        P(("grp", "row"), None, "col", None),
        P("grp", "col"),
        P("grp", "col", None),
        P("grp", ("row", "col"), None),
        P(),
        P(("grp", "col"), "row"),
    )
    out_specs = P(("grp", "col"), "row")
    body = functools.partial(shards, dict(mesh.shape))
    return jax.shard_map(body, mesh=mesh, in_specs=in_specs, out_specs=out_specs, check_vma=False)
```

```python
import functools
import math

import jax
import jax.numpy as jnp
from jax import lax
from jax.experimental import pallas as pl
from jax.experimental.pallas import tpu as pltpu
from jax.sharding import PartitionSpec as P

LAGS = 64
LANES = 128
DIRECT_ROWS = 8
VMEM_GRANT = 16 * 2**20
VMEM = pl.BlockSpec(memory_space=pltpu.VMEM)
HBM = pl.BlockSpec(memory_space=pltpu.HBM)


def in_hbm(value):
    return pltpu.with_memory_space_constraint(value, pltpu.HBM)


def dot_nt(left, right):
    return lax.dot_general(left, right, (((1,), (1,)), ((), ())), preferred_element_type=jnp.float32)


def filter_rows(raw, band):
    rows, length = raw.shape
    block, width = band.shape
    halo = (width - block) // 2
    edge = jnp.zeros((rows, halo), raw.dtype)
    padded = jnp.concatenate([edge, raw, edge], axis=1)
    starts = range(0, length, block)
    stacked = jnp.concatenate([padded[:, start : start + width] for start in starts], axis=0)
    out = dot_nt(stacked.astype(jnp.bfloat16), band)
    pieces = [out[i * rows : (i + 1) * rows] for i in range(len(starts))]
    return jnp.concatenate(pieces[::-1], axis=1)


def source_kernel(
    owner_hbm,
    order_hbm,
    raw_hbm,
    taps_ref,
    kept_ref,
    energy_ref,
    band_ref,
    mine_ref,
    owner_ref,
    order_ref,
    raw_ref,
    row_ref,
    arrived,
):
    windows, count, _ = kept_ref.shape
    owner_copy = pltpu.make_async_copy(owner_hbm, owner_ref, arrived.at[windows])
    order_copy = pltpu.make_async_copy(order_hbm, order_ref, arrived.at[windows + 1])
    copies = [
        pltpu.make_async_copy(raw_hbm.at[window], raw_ref.at[window], arrived.at[window])
        for window in range(windows)
    ]
    for copy in (owner_copy, order_copy, *copies):
        copy.start()
    taps = taps_ref.shape[1]
    half = (taps - 1) // 2
    block, width = band_ref.shape
    row_ref[...] = jnp.zeros_like(row_ref)
    row_ref[:, 0:taps] = taps_ref[...].astype(jnp.float32)
    spread = jnp.broadcast_to(row_ref[...], (LANES, width - LANES))
    part = pltpu.roll(spread, (width - block) // 2 - half, 1, stride=1, stride_axis=0)
    across = lax.broadcasted_iota(jnp.int32, (LANES, LANES), 0)
    down = lax.broadcasted_iota(jnp.int32, (LANES, LANES), 1)
    mirror = jnp.where(across + down == LANES - 1, 1.0, 0.0).astype(jnp.bfloat16)
    part = jnp.dot(mirror, part.astype(jnp.bfloat16), preferred_element_type=jnp.float32)
    empty = jnp.zeros((LANES, LANES), jnp.float32)
    upper = jnp.concatenate([empty, part], axis=1)
    lower = jnp.concatenate([part, empty], axis=1)
    band = jnp.concatenate([upper, lower], axis=0).astype(jnp.bfloat16)
    band_ref[...] = band
    here = lax.axis_index("row")
    owner_copy.wait()
    order_copy.wait()
    mine = sum(jnp.where(owner_ref[0, window] == here, 1 << window, 0) for window in range(windows))
    mine_ref[...] = jnp.full(mine_ref.shape, mine, jnp.int32)
    for window in range(windows):
        place = lax.broadcasted_iota(jnp.int32, (count, count), 0)
        order = jnp.where(owner_ref[0, window] == here, order_ref[window], -1)
        chosen = jnp.where(place == order, 1.0, 0.0).T.astype(jnp.bfloat16)
        copies[window].wait()
        raw = jnp.dot(chosen, raw_ref[window], preferred_element_type=jnp.float32)
        kept = filter_rows(raw.astype(jnp.bfloat16), band).astype(jnp.bfloat16)
        kept_ref[window] = kept
        squares = jnp.square(kept.astype(jnp.float32))
        energy_ref[window] = jnp.sum(squares, axis=1, keepdims=True)


def prepare_sources(block_owner, chan_order, raw, fir_taps):
    windows, count, length = raw.shape
    taps = fir_taps.shape[0]
    block = 2 * LANES
    width = block + 2 * LANES * pl.cdiv((taps - 1) // 2, LANES)
    return pl.pallas_call(
        source_kernel,
        out_shape=(
            jax.ShapeDtypeStruct((windows, count, length), jnp.bfloat16),
            jax.ShapeDtypeStruct((windows, count, 1), jnp.float32),
            jax.ShapeDtypeStruct((block, width), jnp.bfloat16),
            jax.ShapeDtypeStruct((1, LANES), jnp.int32),
        ),
        in_specs=[HBM, HBM, HBM, VMEM],
        out_specs=(VMEM, VMEM, VMEM, VMEM),
        scratch_shapes=[
            pltpu.SMEM((1, windows), jnp.int32),
            pltpu.VMEM((windows, 1, count), jnp.int32),
            pltpu.VMEM((windows, count, length), jnp.bfloat16),
            pltpu.VMEM((1, width - LANES), jnp.float32),
            pltpu.SemaphoreType.DMA((windows + 2,)),
        ],
        cost_estimate=pl.CostEstimate(
            flops=2 * windows * count * length * (count + width),
            bytes_accessed=4 * windows * count * length,
            transcendentals=0,
        ),
        compiler_params=pltpu.CompilerParams(vmem_limit_bytes=VMEM_GRANT),
        name="prepare_sources",
    )(in_hbm(block_owner.T), in_hbm(chan_order), in_hbm(raw), fir_taps.reshape(1, taps))


def window_terms(windows, rec_ref, band_ref, kept_ref, energy_ref, hankel_ref):
    receivers, _, length = rec_ref.shape
    count = len(windows)
    rows = receivers * count
    raw = [rec_ref[q, windows[0] : windows[0] + count].astype(jnp.float32) for q in range(receivers)]
    rec = filter_rows(jnp.concatenate(raw, axis=0), band_ref[...])
    rec = rec.astype(jnp.bfloat16).astype(jnp.float32)
    rec_energy = jnp.sum(jnp.square(rec), axis=1, keepdims=True)
    padded = jnp.concatenate([rec, jnp.zeros((rows, LANES), jnp.float32)], axis=1)
    width = length + LANES
    for i in range(count):
        for q in range(receivers):
            at = q * count + i
            spread = jnp.broadcast_to(padded[at : at + 1], (LAGS, width))
            shifted = pltpu.roll(spread, width - LAGS // 2, 1, stride=1, stride_axis=0)
            hankel_ref[windows[i], q * LAGS : (q + 1) * LAGS] = shifted[:, :length].astype(jnp.bfloat16)
    lane = lax.broadcasted_iota(jnp.int32, (rows, receivers * LAGS), 1) // LAGS
    row = lax.broadcasted_iota(jnp.int32, (rows, receivers * LAGS), 0)
    total = None
    for i, window in enumerate(windows):
        own = jnp.where(row == lane * count + i, rec_energy, 0.0)
        across = jnp.sum(own, axis=0, keepdims=True)
        lagged = dot_nt(kept_ref[window], hankel_ref[window])
        ratio = lagged * lax.rsqrt(energy_ref[window] * across + 1e-06)
        term = jnp.tanh(0.5 * math.sqrt(length) * ratio)
        total = term if total is None else total + term
    return total


def pair_kernel(rec_ref, band_ref, kept_ref, energy_ref, mine_ref, out_ref, hankel_ref, total_ref):
    windows = kept_ref.shape[0]
    terms = functools.partial(
        window_terms,
        rec_ref=rec_ref,
        band_ref=band_ref,
        kept_ref=kept_ref,
        energy_ref=energy_ref,
        hankel_ref=hankel_ref,
    )
    mine = mine_ref[0:1, 0:1][0, 0]
    every = (1 << windows) - 1

    @pl.when(mine == every)
    def _():
        out_ref[...] = terms(range(windows)).astype(out_ref.dtype)

    @pl.when(mine != every)
    def _():
        total_ref[...] = jnp.zeros_like(total_ref)

    for window in range(windows):

        @pl.when((mine != every) & ((mine >> window) & 1 == 1))
        def _():
            total_ref[...] += terms(range(window, window + 1))

    @pl.when(mine != every)
    def _():
        out_ref[...] = total_ref[...].astype(out_ref.dtype)


def pair_terms(rec, band, kept, energy, mine, dtype):
    receivers, windows, length = rec.shape
    count = kept.shape[1]
    return pl.pallas_call(
        pair_kernel,
        out_shape=jax.ShapeDtypeStruct((count, receivers * LAGS), dtype),
        in_specs=[VMEM] * 5,
        out_specs=VMEM,
        scratch_shapes=[
            pltpu.VMEM((windows, receivers * LAGS, length), jnp.bfloat16),
            pltpu.VMEM((count, receivers * LAGS), jnp.float32),
        ],
        cost_estimate=pl.CostEstimate(
            flops=2 * windows * count * length * receivers * LAGS,
            bytes_accessed=4 * windows * count * length,
            transcendentals=windows * count * receivers * LAGS,
        ),
        compiler_params=pltpu.CompilerParams(vmem_limit_bytes=VMEM_GRANT),
        name="pair_terms",
    )(rec, band, kept, energy, mine)


def gather_columns(piece, columns):
    here = lax.axis_index("col")
    if columns & (columns - 1):
        return lax.all_gather(piece, "col", axis=0, tiled=True)
    found = {0: piece}
    for step in range(columns - 1, 0, -1):
        found[step] = lax.ppermute(piece, "col", [(i, i ^ step) for i in range(columns)])
    pieces = [found[step] for step in range(columns)]
    bit = 1
    while bit < columns:
        flip = (here & bit) != 0
        pieces = [jnp.where(flip, pieces[i ^ bit], pieces[i]) for i in range(columns)]
        bit *= 2
    return jnp.concatenate(pieces, axis=0)


def shards(mesh_shape, src_raw, block_owner, chan_order, rec_raw, fir_taps, stacks):
    rows, columns = mesh_shape["row"], mesh_shape["col"]
    prepared = prepare_sources(block_owner, chan_order, src_raw[0], fir_taps)
    receivers = gather_columns(jnp.swapaxes(rec_raw, 0, 1), columns)
    receivers, prepared = lax.optimization_barrier((receivers, prepared))
    kept, energy, band, mine = prepared
    terms = functools.partial(pair_terms, band=band, kept=kept, energy=energy, mine=mine)
    if rows > DIRECT_ROWS:
        everyone = lax.all_gather(receivers, "row", axis=0)
        parts = lax.map(lambda rec: terms(rec, dtype=jnp.bfloat16), everyone)
        parts = lax.all_to_all(parts, "row", 0, 0, tiled=True)
        return stacks + jnp.sum(parts.astype(jnp.float32), axis=0)

    def partner(i, step):
        return i ^ step if rows & (rows - 1) == 0 else (i + step) % rows

    order = [1, *range(rows - 1, 1, -1)]
    arrived = {}
    for step in order:
        pairs = [(partner(i, step), i) for i in range(rows)]
        arrived[step] = lax.ppermute(receivers, "row", pairs)
    parts = []
    for step in order:
        pairs = [(i, partner(i, step)) for i in range(rows)]
        parts.append(lax.ppermute(terms(arrived[step], dtype=jnp.bfloat16), "row", pairs))
    total = stacks + terms(receivers, dtype=jnp.float32)
    for part in parts:
        total = total + part.astype(jnp.float32)
    return total


def solution(mesh):
    in_specs = (
        P(("grp", "row"), None, "col", None),
        P("grp", "col"),
        P("grp", "col", None),
        P("grp", ("row", "col"), None),
        P(),
        P(("grp", "col"), "row"),
    )
    out_specs = P(("grp", "col"), "row")
    body = functools.partial(shards, dict(mesh.shape))
    return jax.shard_map(body, mesh=mesh, in_specs=in_specs, out_specs=out_specs, check_vma=False)
```

```python
import functools
import math

import jax
import jax.numpy as jnp
from jax import lax
from jax.experimental import pallas as pl
from jax.experimental.pallas import tpu as pltpu
from jax.sharding import PartitionSpec as P

LAGS = 64
LANES = 128
DIRECT_ROWS = 8
VMEM_GRANT = 16 * 2**20
VMEM = pl.BlockSpec(memory_space=pltpu.VMEM)
HBM = pl.BlockSpec(memory_space=pltpu.HBM)


def in_hbm(value):
    return pltpu.with_memory_space_constraint(value, pltpu.HBM)


def dot_nt(left, right):
    return lax.dot_general(left, right, (((1,), (1,)), ((), ())), preferred_element_type=jnp.float32)


def dot_nn(left, right):
    return jnp.dot(left, right, preferred_element_type=jnp.float32)


def filter_rows(raw, band, dot):
    rows, length = raw.shape
    width, block = max(band.shape), min(band.shape)
    halo = (width - block) // 2
    edge = jnp.zeros((rows, halo), raw.dtype)
    padded = jnp.concatenate([edge, raw, edge], axis=1)
    starts = range(0, length, block)
    stacked = jnp.concatenate([padded[:, start : start + width] for start in starts], axis=0)
    out = dot(stacked.astype(jnp.bfloat16), band)
    pieces = [out[i * rows : (i + 1) * rows] for i in range(len(starts))]
    return jnp.concatenate(pieces[::-1], axis=1)


def source_kernel(
    owner_hbm,
    order_hbm,
    raw_hbm,
    taps_ref,
    kept_ref,
    energy_ref,
    band_ref,
    mine_ref,
    owner_ref,
    order_ref,
    raw_ref,
    row_ref,
    arrived,
):
    windows, count, _ = kept_ref.shape
    owner_copy = pltpu.make_async_copy(owner_hbm, owner_ref, arrived.at[windows])
    order_copy = pltpu.make_async_copy(order_hbm, order_ref, arrived.at[windows + 1])
    copies = [
        pltpu.make_async_copy(raw_hbm.at[window], raw_ref.at[window], arrived.at[window])
        for window in range(windows)
    ]
    for copy in (owner_copy, order_copy, *copies):
        copy.start()
    taps = taps_ref.shape[1]
    half = (taps - 1) // 2
    width, block = band_ref.shape
    row_ref[...] = jnp.zeros_like(row_ref)
    row_ref[:, 0:taps] = taps_ref[...].astype(jnp.float32)
    spread = jnp.broadcast_to(row_ref[...], (LANES, width - LANES))
    part = pltpu.roll(spread, (width - block) // 2 - half, 1, stride=1, stride_axis=0)
    across = lax.broadcasted_iota(jnp.int32, (LANES, LANES), 0)
    down = lax.broadcasted_iota(jnp.int32, (LANES, LANES), 1)
    mirror = jnp.where(across + down == LANES - 1, 1.0, 0.0).astype(jnp.bfloat16)
    part = jnp.dot(mirror, part.astype(jnp.bfloat16), preferred_element_type=jnp.float32)
    empty = jnp.zeros((LANES, LANES), jnp.float32)
    upper = jnp.concatenate([empty, part], axis=1)
    lower = jnp.concatenate([part, empty], axis=1)
    band = jnp.concatenate([upper, lower], axis=0).astype(jnp.bfloat16)
    upper = jnp.concatenate([empty, part.T], axis=0)
    lower = jnp.concatenate([part.T, empty], axis=0)
    band_ref[...] = jnp.concatenate([upper, lower], axis=1).astype(jnp.bfloat16)
    here = lax.axis_index("row")
    owner_copy.wait()
    order_copy.wait()
    mine = sum(jnp.where(owner_ref[0, window] == here, 1 << window, 0) for window in range(windows))
    mine_ref[...] = jnp.full(mine_ref.shape, mine, jnp.int32)
    for window in range(windows):
        place = lax.broadcasted_iota(jnp.int32, (count, count), 0)
        order = jnp.where(owner_ref[0, window] == here, order_ref[window], -1)
        chosen = jnp.where(place == order, 1.0, 0.0).T.astype(jnp.bfloat16)
        copies[window].wait()
        raw = jnp.dot(chosen, raw_ref[window], preferred_element_type=jnp.float32)
        kept = filter_rows(raw.astype(jnp.bfloat16), band, dot_nt).astype(jnp.bfloat16)
        kept_ref[window] = kept
        squares = jnp.square(kept.astype(jnp.float32))
        energy_ref[window] = jnp.sum(squares, axis=1, keepdims=True)


def prepare_sources(block_owner, chan_order, raw, fir_taps):
    windows, count, length = raw.shape
    taps = fir_taps.shape[0]
    block = 2 * LANES
    width = block + 2 * LANES * pl.cdiv((taps - 1) // 2, LANES)
    return pl.pallas_call(
        source_kernel,
        out_shape=(
            jax.ShapeDtypeStruct((windows, count, length), jnp.bfloat16),
            jax.ShapeDtypeStruct((windows, count, 1), jnp.float32),
            jax.ShapeDtypeStruct((width, block), jnp.bfloat16),
            jax.ShapeDtypeStruct((1, LANES), jnp.int32),
        ),
        in_specs=[HBM, HBM, HBM, VMEM],
        out_specs=(VMEM, VMEM, VMEM, VMEM),
        scratch_shapes=[
            pltpu.SMEM((1, windows), jnp.int32),
            pltpu.VMEM((windows, 1, count), jnp.int32),
            pltpu.VMEM((windows, count, length), jnp.bfloat16),
            pltpu.VMEM((1, width - LANES), jnp.float32),
            pltpu.SemaphoreType.DMA((windows + 2,)),
        ],
        cost_estimate=pl.CostEstimate(
            flops=2 * windows * count * length * (count + width),
            bytes_accessed=4 * windows * count * length,
            transcendentals=0,
        ),
        compiler_params=pltpu.CompilerParams(vmem_limit_bytes=VMEM_GRANT),
        name="prepare_sources",
    )(in_hbm(block_owner.T), in_hbm(chan_order), in_hbm(raw), fir_taps.reshape(1, taps))


def window_terms(windows, rec_ref, band_ref, kept_ref, energy_ref, hankel_ref):
    receivers, every, length = rec_ref.shape
    rows = receivers * every
    raw = jnp.concatenate([rec_ref[q].astype(jnp.float32) for q in range(receivers)], axis=0)
    rec = filter_rows(raw, band_ref[...], dot_nn)
    rec = rec.astype(jnp.bfloat16).astype(jnp.float32)
    rec_energy = jnp.sum(jnp.square(rec), axis=1, keepdims=True)
    padded = jnp.concatenate([rec, jnp.zeros((rows, LANES), jnp.float32)], axis=1)
    width = length + LANES
    for window in windows:
        for q in range(receivers):
            at = q * every + window
            spread = jnp.broadcast_to(padded[at : at + 1], (LAGS, width))
            shifted = pltpu.roll(spread, width - LAGS // 2, 1, stride=1, stride_axis=0)
            hankel_ref[window, q * LAGS : (q + 1) * LAGS] = shifted[:, :length].astype(jnp.bfloat16)
    lane = lax.broadcasted_iota(jnp.int32, (rows, receivers * LAGS), 1) // LAGS
    row = lax.broadcasted_iota(jnp.int32, (rows, receivers * LAGS), 0)
    total = None
    for window in windows:
        own = jnp.where(row == lane * every + window, rec_energy, 0.0)
        across = jnp.sum(own, axis=0, keepdims=True)
        lagged = dot_nt(kept_ref[window], hankel_ref[window])
        ratio = lagged * lax.rsqrt(energy_ref[window] * across + 1e-06)
        term = jnp.tanh(0.5 * math.sqrt(length) * ratio)
        total = term if total is None else total + term
    return total


def pair_kernel(rec_ref, band_ref, kept_ref, energy_ref, mine_ref, out_ref, hankel_ref, total_ref):
    windows = kept_ref.shape[0]
    terms = functools.partial(
        window_terms,
        rec_ref=rec_ref,
        band_ref=band_ref,
        kept_ref=kept_ref,
        energy_ref=energy_ref,
        hankel_ref=hankel_ref,
    )
    mine = mine_ref[0:1, 0:1][0, 0]
    every = (1 << windows) - 1

    @pl.when(mine == 0)
    def _():
        out_ref[...] = jnp.zeros_like(out_ref)

    @pl.when(mine == every)
    def _():
        out_ref[...] = terms(range(windows)).astype(out_ref.dtype)

    if windows == 2:
        for window in range(windows):

            @pl.when(mine == 1 << window)
            def _():
                out_ref[...] = terms([window]).astype(out_ref.dtype)

        return

    @pl.when((mine != 0) & (mine != every))
    def _():
        total_ref[...] = jnp.zeros_like(total_ref)
        for window in range(windows):

            @pl.when((mine >> window) & 1 == 1)
            def _():
                total_ref[...] += terms([window])

        out_ref[...] = total_ref[...].astype(out_ref.dtype)


def pair_terms(rec, band, kept, energy, mine, dtype):
    receivers, windows, length = rec.shape
    count = kept.shape[1]
    return pl.pallas_call(
        pair_kernel,
        out_shape=jax.ShapeDtypeStruct((count, receivers * LAGS), dtype),
        in_specs=[VMEM] * 5,
        out_specs=VMEM,
        scratch_shapes=[
            pltpu.VMEM((windows, receivers * LAGS, length), jnp.bfloat16),
            pltpu.VMEM((count, receivers * LAGS), jnp.float32),
        ],
        cost_estimate=pl.CostEstimate(
            flops=2 * windows * count * length * receivers * LAGS,
            bytes_accessed=4 * windows * count * length,
            transcendentals=windows * count * receivers * LAGS,
        ),
        compiler_params=pltpu.CompilerParams(vmem_limit_bytes=VMEM_GRANT),
        name="pair_terms",
    )(rec, band, kept, energy, mine)


def gather_columns(piece, columns):
    here = lax.axis_index("col")
    if columns & (columns - 1):
        return lax.all_gather(piece, "col", axis=0, tiled=True)
    found = {0: piece}
    for step in range(columns - 1, 0, -1):
        found[step] = lax.ppermute(piece, "col", [(i, i ^ step) for i in range(columns)])
    pieces = [found[step] for step in range(columns)]
    bit = 1
    while bit < columns:
        flip = (here & bit) != 0
        pieces = [jnp.where(flip, pieces[i ^ bit], pieces[i]) for i in range(columns)]
        bit *= 2
    return jnp.concatenate(pieces, axis=0)


def shards(mesh_shape, src_raw, block_owner, chan_order, rec_raw, fir_taps, stacks):
    rows, columns = mesh_shape["row"], mesh_shape["col"]
    prepared = prepare_sources(block_owner, chan_order, src_raw[0], fir_taps)
    receivers = gather_columns(jnp.swapaxes(rec_raw, 0, 1), columns)
    receivers, prepared = lax.optimization_barrier((receivers, prepared))
    kept, energy, band, mine = prepared
    terms = functools.partial(pair_terms, band=band, kept=kept, energy=energy, mine=mine)
    if rows > DIRECT_ROWS:
        everyone = lax.all_gather(receivers, "row", axis=0)
        parts = lax.map(lambda rec: terms(rec, dtype=jnp.bfloat16), everyone)
        parts = lax.all_to_all(parts, "row", 0, 0, tiled=True)
        return stacks + jnp.sum(parts.astype(jnp.float32), axis=0)

    def partner(i, step):
        return i ^ step if rows & (rows - 1) == 0 else (i + step) % rows

    order = [1, *range(rows - 1, 1, -1)]
    arrived = {}
    for step in order:
        pairs = [(partner(i, step), i) for i in range(rows)]
        arrived[step] = lax.ppermute(receivers, "row", pairs)
    parts = []
    for step in order:
        pairs = [(i, partner(i, step)) for i in range(rows)]
        parts.append(lax.ppermute(terms(arrived[step], dtype=jnp.bfloat16), "row", pairs))
    total = stacks + terms(receivers, dtype=jnp.float32)
    for part in parts:
        total = total + part.astype(jnp.float32)
    return total


def solution(mesh):
    in_specs = (
        P(("grp", "row"), None, "col", None),
        P("grp", "col"),
        P("grp", "col", None),
        P("grp", ("row", "col"), None),
        P(),
        P(("grp", "col"), "row"),
    )
    out_specs = P(("grp", "col"), "row")
    body = functools.partial(shards, dict(mesh.shape))
    return jax.shard_map(body, mesh=mesh, in_specs=in_specs, out_specs=out_specs, check_vma=False)
```

```python
import functools
import math

import jax
import jax.numpy as jnp
from jax import lax
from jax.experimental import pallas as pl
from jax.experimental.pallas import tpu as pltpu
from jax.sharding import PartitionSpec as P

LAGS = 64
LANES = 128
DIRECT_ROWS = 8
VMEM_GRANT = 16 * 2**20
VMEM = pl.BlockSpec(memory_space=pltpu.VMEM)
HBM = pl.BlockSpec(memory_space=pltpu.HBM)


def in_hbm(value):
    return pltpu.with_memory_space_constraint(value, pltpu.HBM)


def dot_nt(left, right):
    return lax.dot_general(left, right, (((1,), (1,)), ((), ())), preferred_element_type=jnp.float32)


def dot_nn(left, right):
    return jnp.dot(left, right, preferred_element_type=jnp.float32)


def filter_rows(raw, band, dot):
    rows, length = raw.shape
    width, block = max(band.shape), min(band.shape)
    halo = (width - block) // 2
    edge = jnp.zeros((rows, halo), raw.dtype)
    padded = jnp.concatenate([edge, raw, edge], axis=1)
    starts = range(0, length, block)
    stacked = jnp.concatenate([padded[:, start : start + width] for start in starts], axis=0)
    out = dot(stacked.astype(jnp.bfloat16), band)
    pieces = [out[i * rows : (i + 1) * rows] for i in range(len(starts))]
    return jnp.concatenate(pieces[::-1], axis=1)


def source_kernel(
    owner_hbm,
    order_hbm,
    raw_hbm,
    taps_ref,
    kept_ref,
    energy_ref,
    band_ref,
    mine_ref,
    owner_ref,
    order_ref,
    raw_ref,
    row_ref,
    arrived,
):
    windows, count, _ = kept_ref.shape
    owner_copy = pltpu.make_async_copy(owner_hbm, owner_ref, arrived.at[windows])
    order_copy = pltpu.make_async_copy(order_hbm, order_ref, arrived.at[windows + 1])
    copies = [
        pltpu.make_async_copy(raw_hbm.at[window], raw_ref.at[window], arrived.at[window])
        for window in range(windows)
    ]
    for copy in (owner_copy, order_copy, *copies):
        copy.start()
    taps = taps_ref.shape[1]
    half = (taps - 1) // 2
    width, block = band_ref.shape
    row_ref[...] = jnp.zeros_like(row_ref)
    row_ref[:, 0:taps] = taps_ref[...].astype(jnp.float32)
    spread = jnp.broadcast_to(row_ref[...], (LANES, width - LANES))
    part = pltpu.roll(spread, (width - block) // 2 - half, 1, stride=1, stride_axis=0)
    across = lax.broadcasted_iota(jnp.int32, (LANES, LANES), 0)
    down = lax.broadcasted_iota(jnp.int32, (LANES, LANES), 1)
    mirror = jnp.where(across + down == LANES - 1, 1.0, 0.0).astype(jnp.bfloat16)
    part = jnp.dot(mirror, part.astype(jnp.bfloat16), preferred_element_type=jnp.float32)
    empty = jnp.zeros((LANES, LANES), jnp.float32)
    upper = jnp.concatenate([empty, part], axis=1)
    lower = jnp.concatenate([part, empty], axis=1)
    band = jnp.concatenate([upper, lower], axis=0).astype(jnp.bfloat16)
    upper = jnp.concatenate([empty, part.T], axis=0)
    lower = jnp.concatenate([part.T, empty], axis=0)
    band_ref[...] = jnp.concatenate([upper, lower], axis=1).astype(jnp.bfloat16)
    here = lax.axis_index("row")
    owner_copy.wait()
    order_copy.wait()
    mine = sum(jnp.where(owner_ref[0, window] == here, 1 << window, 0) for window in range(windows))
    mine_ref[...] = jnp.full(mine_ref.shape, mine, jnp.int32)
    for window in range(windows):
        place = lax.broadcasted_iota(jnp.int32, (count, count), 0)
        order = jnp.where(owner_ref[0, window] == here, order_ref[window], -1)
        chosen = jnp.where(place == order, 1.0, 0.0).T.astype(jnp.bfloat16)
        copies[window].wait()
        raw = jnp.dot(chosen, raw_ref[window], preferred_element_type=jnp.float32)
        kept = filter_rows(raw.astype(jnp.bfloat16), band, dot_nt).astype(jnp.bfloat16)
        kept_ref[window] = kept
        squares = jnp.square(kept.astype(jnp.float32))
        energy_ref[window] = jnp.sum(squares, axis=1, keepdims=True)


def prepare_sources(block_owner, chan_order, raw, fir_taps):
    windows, count, length = raw.shape
    taps = fir_taps.shape[0]
    block = 2 * LANES
    width = block + 2 * LANES * pl.cdiv((taps - 1) // 2, LANES)
    return pl.pallas_call(
        source_kernel,
        out_shape=(
            jax.ShapeDtypeStruct((windows, count, length), jnp.bfloat16),
            jax.ShapeDtypeStruct((windows, count, 1), jnp.float32),
            jax.ShapeDtypeStruct((width, block), jnp.bfloat16),
            jax.ShapeDtypeStruct((1, LANES), jnp.int32),
        ),
        in_specs=[HBM, HBM, HBM, VMEM],
        out_specs=(VMEM, VMEM, VMEM, VMEM),
        scratch_shapes=[
            pltpu.SMEM((1, windows), jnp.int32),
            pltpu.VMEM((windows, 1, count), jnp.int32),
            pltpu.VMEM((windows, count, length), jnp.bfloat16),
            pltpu.VMEM((1, width - LANES), jnp.float32),
            pltpu.SemaphoreType.DMA((windows + 2,)),
        ],
        cost_estimate=pl.CostEstimate(
            flops=2 * windows * count * length * (count + width),
            bytes_accessed=4 * windows * count * length,
            transcendentals=0,
        ),
        compiler_params=pltpu.CompilerParams(vmem_limit_bytes=VMEM_GRANT),
        name="prepare_sources",
    )(in_hbm(block_owner.T), in_hbm(chan_order), in_hbm(raw), fir_taps.reshape(1, taps))


def window_terms(windows, rec_ref, band_ref, kept_ref, energy_ref, hankel_ref):
    receivers, every, length = rec_ref.shape
    rows = receivers * every
    raw = jnp.concatenate([rec_ref[q].astype(jnp.float32) for q in range(receivers)], axis=0)
    rec = filter_rows(raw, band_ref[...], dot_nn)
    rec = rec.astype(jnp.bfloat16).astype(jnp.float32)
    rec_energy = jnp.sum(jnp.square(rec), axis=1, keepdims=True)
    padded = jnp.concatenate([rec, jnp.zeros((rows, LANES), jnp.float32)], axis=1)
    width = length + LANES
    for window in windows:
        for q in range(receivers):
            at = q * every + window
            spread = jnp.broadcast_to(padded[at : at + 1], (LAGS, width))
            shifted = pltpu.roll(spread, width - LAGS // 2, 1, stride=1, stride_axis=0)
            hankel_ref[window, q * LAGS : (q + 1) * LAGS] = shifted[:, :length].astype(jnp.bfloat16)
    lane = lax.broadcasted_iota(jnp.int32, (rows, receivers * LAGS), 1) // LAGS
    row = lax.broadcasted_iota(jnp.int32, (rows, receivers * LAGS), 0)
    total = None
    for window in windows:
        own = jnp.where(row == lane * every + window, rec_energy, 0.0)
        across = jnp.sum(own, axis=0, keepdims=True)
        lagged = dot_nt(kept_ref[window], hankel_ref[window])
        ratio = lagged * lax.rsqrt(energy_ref[window] * across + 1e-06)
        term = jnp.tanh(0.5 * math.sqrt(length) * ratio)
        total = term if total is None else total + term
    return total


def pair_kernel(rec_ref, band_ref, kept_ref, energy_ref, mine_ref, out_ref, hankel_ref, total_ref):
    windows = kept_ref.shape[0]
    terms = functools.partial(
        window_terms,
        rec_ref=rec_ref,
        band_ref=band_ref,
        kept_ref=kept_ref,
        energy_ref=energy_ref,
        hankel_ref=hankel_ref,
    )
    mine = mine_ref[0:1, 0:1][0, 0]
    every = (1 << windows) - 1

    @pl.when(mine == 0)
    def _():
        out_ref[...] = jnp.zeros_like(out_ref)

    @pl.when(mine == every)
    def _():
        out_ref[...] = terms(range(windows)).astype(out_ref.dtype)

    if windows == 2:
        for window in range(windows):

            @pl.when(mine == 1 << window)
            def _():
                out_ref[...] = terms([window]).astype(out_ref.dtype)

        return

    @pl.when((mine != 0) & (mine != every))
    def _():
        total_ref[...] = jnp.zeros_like(total_ref)
        for window in range(windows):

            @pl.when((mine >> window) & 1 == 1)
            def _():
                total_ref[...] += terms([window])

        out_ref[...] = total_ref[...].astype(out_ref.dtype)


def pair_terms(rec, band, kept, energy, mine, dtype):
    receivers, windows, length = rec.shape
    count = kept.shape[1]
    return pl.pallas_call(
        pair_kernel,
        out_shape=jax.ShapeDtypeStruct((count, receivers * LAGS), dtype),
        in_specs=[VMEM] * 5,
        out_specs=VMEM,
        scratch_shapes=[
            pltpu.VMEM((windows, receivers * LAGS, length), jnp.bfloat16),
            pltpu.VMEM((count, receivers * LAGS), jnp.float32),
        ],
        cost_estimate=pl.CostEstimate(
            flops=2 * windows * count * length * receivers * LAGS,
            bytes_accessed=4 * windows * count * length,
            transcendentals=windows * count * receivers * LAGS,
        ),
        compiler_params=pltpu.CompilerParams(vmem_limit_bytes=VMEM_GRANT),
        name="pair_terms",
    )(rec, band, kept, energy, mine)


def gather_columns(piece, columns):
    here = lax.axis_index("col")
    if columns & (columns - 1):
        return lax.all_gather(piece, "col", axis=0, tiled=True)
    found = {0: piece}
    for step in range(columns - 1, 0, -1):
        found[step] = lax.ppermute(piece, "col", [(i, i ^ step) for i in range(columns)])
    pieces = [found[step] for step in range(columns)]
    bit = 1
    while bit < columns:
        flip = (here & bit) != 0
        pieces = [jnp.where(flip, pieces[i ^ bit], pieces[i]) for i in range(columns)]
        bit *= 2
    return jnp.concatenate(pieces, axis=0)


def far_first(rows):
    return [*range(2, rows), 1]


def shards(mesh_shape, src_raw, block_owner, chan_order, rec_raw, fir_taps, stacks):
    rows, columns = mesh_shape["row"], mesh_shape["col"]
    prepared = prepare_sources(block_owner, chan_order, src_raw[0], fir_taps)
    receivers = gather_columns(jnp.swapaxes(rec_raw, 0, 1), columns)
    receivers, prepared = lax.optimization_barrier((receivers, prepared))
    kept, energy, band, mine = prepared
    terms = functools.partial(pair_terms, band=band, kept=kept, energy=energy, mine=mine)
    if rows > DIRECT_ROWS:
        everyone = lax.all_gather(receivers, "row", axis=0)
        parts = lax.map(lambda rec: terms(rec, dtype=jnp.bfloat16), everyone)
        parts = lax.all_to_all(parts, "row", 0, 0, tiled=True)
        return stacks + jnp.sum(parts.astype(jnp.float32), axis=0)

    def partner(i, step):
        return i ^ step if rows & (rows - 1) == 0 else (i + step) % rows

    def send(value, step):
        return lax.ppermute(value, "row", [(i, partner(i, step)) for i in range(rows)])

    def fetch(value, step):
        return lax.ppermute(value, "row", [(partner(i, step), i) for i in range(rows)])

    order = far_first(rows)
    arrived = {step: fetch(receivers, step) for step in order}
    parts = [send(terms(arrived[step], dtype=jnp.bfloat16), step) for step in order]
    total = stacks + terms(receivers, dtype=jnp.float32)
    for part in parts:
        total = total + part.astype(jnp.float32)
    return total


def solution(mesh):
    in_specs = (
        P(("grp", "row"), None, "col", None),
        P("grp", "col"),
        P("grp", "col", None),
        P("grp", ("row", "col"), None),
        P(),
        P(("grp", "col"), "row"),
    )
    out_specs = P(("grp", "col"), "row")

    def body(*args):
        return shards(dict(mesh.shape), *args)

    return jax.shard_map(body, mesh=mesh, in_specs=in_specs, out_specs=out_specs, check_vma=False)
```
